256 devices in a mesh: rows: 8 (over y, x_lo), cols: 32 (over z, x_hi, core).
Axes of the slice: x: 4 (x_hi: 2, x_lo: 2; x = x_hi * 2 + x_lo), y: 4, z: 8, core: 2. Of those that a mesh axis runs over, the one named last changes fastest.
Arguments:
- counts: bfloat16 [4096, 262144], P('rows', 'cols'), may hold values from 0 to 12, as said below
- start_a: float32 [4096, 128], P(('rows', 'cols')), may hold values from -0.4 to 0.4
- start_b: float32 [16384, 128], P(('cols', 'rows')), may hold values from -0.4 to 0.4
- start_c: float32 [16, 128], replicated, may hold values from -0.4 to 0.4
Outputs:
- factor_a: float32 [4096, 128], P(('rows', 'cols'))
- factor_b: float32 [16384, 128], P(('cols', 'rows'))
- factor_c: float32 [16, 128], replicated
The draws below stay inside these ranges and needn't reach their ends.
Inputs may be any that keep to these rules, and one draw needn't show every extreme that they name: counts holds whole numbers.
All inputs are finite; a program needn't handle non-finite values.
Results may differ from the reference program's by a relative error of at most 0.009.
Values may be sent and summed in bfloat16 or wider, within the bound.
No kernel may reach another device: no remote copies, remote signals or barrier semaphores. Data moves between devices by JAX's collectives and lax.ppermute only.
A program may use at most 128 MiB of HBM per device.

```python
import math
import jax
import jax.numpy as jnp
from jax import lax

R = 128
K = 16
ITERS = 2
I = 4096
J = 16384


def draw_counts(key, part):
    keys = jax.random.split(key, 4)
    rate_first = jax.random.randint(keys[0], (I, 1, 1), 0, 5)
    rate_second = jax.random.randint(keys[1], (1, J, 1), 0, 5)
    rate_third = jax.random.randint(keys[2], (1, 1, K), 0, 5)
    ceiling = 1 + rate_first + rate_second + rate_third
    values = jax.random.randint(keys[3], (I, J, K), 0, ceiling)
    values = values.at[0, 0, 0].set(12)
    return values.reshape(I, J * K).astype(jnp.float32).astype(jnp.bfloat16)


def shard_levels(key, shape, shards, least, top_value):
    factor_of = 1.0
    for position, blocks in shards:
        steps = jax.random.uniform(jax.random.fold_in(jax.random.fold_in(key, 6), position), (blocks,), jnp.float32, least / len(shards), top_value / len(shards))
        factor_of = factor_of * jnp.repeat(jnp.exp(steps), shape[position] // blocks).reshape((-1,) + (1,) * (len(shape) - 1 - position))
    return factor_of


def setup_inputs(seed: int = 0) -> dict:
    seeds = jax.random.split(jax.random.key(seed), 5)
    counts = draw_counts(jax.random.fold_in(seeds[4], 71), 0)
    start_a = jnp.clip(jax.random.uniform(seeds[1], (I, R), jnp.float32, -0.4, 0.4) * shard_levels(seeds[1], (I, R), ((0, 256),), -0.4, 0.0), -0.4, 0.4)
    start_b = jnp.clip(jax.random.uniform(seeds[2], (J, R), jnp.float32, -0.4, 0.4) * shard_levels(seeds[2], (J, R), ((0, 256),), -0.4, 0.0), -0.4, 0.4)
    start_c = jnp.clip(jax.random.uniform(seeds[3], (K, R), jnp.float32, -0.4, 0.4), -0.4, 0.4)
    return {"counts": counts, "start_a": start_a, "start_b": start_b, "start_c": start_c}


def one_step(counts, whole_a, whole_b, whole_c):
    low_a = whole_a.astype(jnp.bfloat16)
    low_b = whole_b.astype(jnp.bfloat16)
    scaled = (low_b.astype(jnp.float32)[:, None, :] * whole_c[None, :, :]).astype(jnp.bfloat16)
    scaled = scaled.reshape(J * K, R)
    block_rows = math.gcd(I, 256)
    flat = counts.reshape(I // block_rows, block_rows, J * K)
    blocks_a = low_a.reshape(I // block_rows, block_rows, R)

    def visit(mixed, pair):
        values, rows_a = pair
        log_rate = lax.dot_general(rows_a, scaled, (((1,), (1,)), ((), ())), preferred_element_type=jnp.float32)
        residual = (jnp.exp(log_rate) - values.astype(jnp.float32)).astype(jnp.bfloat16)
        grad_rows = jnp.dot(residual, scaled, preferred_element_type=jnp.float32)
        mixed = mixed + lax.dot_general(residual, rows_a, (((0,), (0,)), ((), ())), preferred_element_type=jnp.float32)
        return (mixed, grad_rows)
    mixed, grad_a = lax.scan(visit, jnp.zeros((J * K, R), jnp.float32), (flat, blocks_a))
    grad_a = grad_a.reshape(I, R)
    mixed = mixed.reshape(J, K, R)
    grad_b = lax.optimization_barrier(jnp.sum(mixed * whole_c[None, :, :], axis=1))
    grad_c = lax.optimization_barrier(jnp.sum(mixed * low_b.astype(jnp.float32)[:, None, :], axis=0))
    whole_a = whole_a - 0.3 / math.sqrt(J * K) * grad_a
    whole_b = whole_b - 0.3 / math.sqrt(I * K) * grad_b
    whole_c = whole_c - 0.3 / math.sqrt(I * J) * grad_c
    return (whole_a, whole_b, whole_c)

def reference(counts, start_a, start_b, start_c):
    whole_a, whole_b, whole_c = (start_a, start_b, start_c)
    for iteration in range(ITERS):
        whole_a, whole_b, whole_c = one_step(counts, whole_a, whole_b, whole_c)
    return (whole_a, whole_b, whole_c)
```

```python
import functools
import math

import jax
import jax.numpy as jnp
from jax import lax
from jax.experimental import pallas as pl
from jax.experimental.pallas import tpu as pltpu
from jax.sharding import PartitionSpec as P

ITERS = 2
BF16 = jnp.bfloat16
F32 = jnp.float32
TILE = 1024


def grads_body(n_ref, a_ref, b_ref, c_ref, ga_ref, gb_ref, gc_ref):
    depth, rank = c_ref.shape
    flat = n_ref.shape[1]
    tile = math.gcd(flat, TILE)
    wide = tile // depth
    low_a = a_ref[...]
    c = c_ref[...]
    ga_ref[...] = jnp.zeros_like(ga_ref)
    gc_ref[...] = jnp.zeros_like(gc_ref)
    for q in range(flat // tile):
        columns = slice(q * tile, (q + 1) * tile)
        here = slice(q * wide, (q + 1) * wide)
        low_b = b_ref[here].astype(F32)
        scaled = (low_b[:, None, :] * c[None]).astype(BF16).reshape(tile, rank)
        log_rate = lax.dot_general(
            low_a, scaled, (((1,), (1,)), ((), ())), preferred_element_type=F32
        )
        residual = (jnp.exp(log_rate) - n_ref[:, columns].astype(F32)).astype(BF16)
        mixed = lax.dot_general(
            residual, low_a, (((0,), (0,)), ((), ())), preferred_element_type=F32
        ).reshape(wide, depth, rank)
        gb_ref[here] = jnp.sum(mixed * c[None], axis=1)
        gc_ref[...] += jnp.sum(mixed * low_b[:, None, :], axis=0)
        ga_ref[...] += jnp.dot(residual, scaled, preferred_element_type=F32)


def grads(counts, low_a, low_b, c):
    rows, flat = counts.shape
    depth, rank = c.shape
    whole = pl.BlockSpec(memory_space=pltpu.VMEM)
    return pl.pallas_call(
        grads_body,
        in_specs=[whole] * 4,
        out_specs=[whole] * 3,
        out_shape=[
            jax.ShapeDtypeStruct((rows, rank), F32),
            jax.ShapeDtypeStruct((flat // depth, rank), F32),
            jax.ShapeDtypeStruct((depth, rank), F32),
        ],
        compiler_params=pltpu.CompilerParams(vmem_limit_bytes=20 << 20),
        cost_estimate=pl.CostEstimate(
            flops=6 * rows * flat * rank,
            transcendentals=rows * flat,
            bytes_accessed=2 * rows * flat,
        ),
    )(counts, low_a, low_b, c)


def gather(piece, axis):
    n = lax.axis_size(axis)
    out = lax.all_to_all(jnp.broadcast_to(piece[None], (n, *piece.shape)), axis, 0, 0)
    return out.reshape(n * piece.shape[0], piece.shape[1])


def reduce_with(whole, extra, axis):
    n = lax.axis_size(axis)
    rows = whole.shape[0] // n
    pieces = whole.astype(BF16).reshape(n, rows, whole.shape[1])
    extras = jnp.broadcast_to(extra.astype(BF16)[None], (n, *extra.shape))
    got = lax.all_to_all(jnp.concatenate([pieces, extras], axis=1), axis, 0, 0)
    total = jnp.sum(got.astype(F32), axis=0)
    return total[:rows], total[rows:]


def local(counts, start_a, start_b, start_c):
    rows_here, flat_width = counts.shape
    depth = start_c.shape[0]
    cols_here = flat_width // depth
    total_i = rows_here * lax.axis_size("rows")
    total_j = cols_here * lax.axis_size("cols")
    rate_a = 0.3 / math.sqrt(total_j * depth)
    rate_b = 0.3 / math.sqrt(total_i * depth)
    rate_c = 0.3 / math.sqrt(total_i * total_j)
    local_a, local_b, shared_c = (start_a, start_b, start_c)
    for iteration in range(ITERS):
        low_b = gather(local_b.astype(BF16), "rows")
        low_a = gather(local_a.astype(BF16), "cols")
        grad_a, grad_b, grad_c = grads(counts, low_a, low_b, shared_c)
        summed_b, part_c = reduce_with(grad_b, grad_c, "rows")
        summed_a, summed_c = reduce_with(grad_a, part_c, "cols")
        local_a = local_a - rate_a * summed_a
        local_b = local_b - rate_b * summed_b
        shared_c = shared_c - rate_c * summed_c
    return (local_a, local_b, shared_c)


def solution(mesh):
    placed = (P("rows", "cols"), P(("rows", "cols"), None), P(("cols", "rows"), None), P())
    return jax.shard_map(
        local,
        mesh=mesh,
        in_specs=placed,
        out_specs=(P(("rows", "cols"), None), P(("cols", "rows"), None), P()),
        check_vma=False,
    )
```

```python
import functools
import math

import jax
import jax.numpy as jnp
from jax import lax
from jax.experimental import pallas as pl
from jax.experimental.pallas import tpu as pltpu
from jax.sharding import PartitionSpec as P

ITERS = 2
BF16 = jnp.bfloat16
F32 = jnp.float32


def grads_body(last, n_ref, a_ref, *refs):
    b_refs, (c_ref, xa_ref, xb_ref, acc_ref, held_ref, sems) = refs[:-6], refs[-6:]
    depth, rank = c_ref.shape
    flat = n_ref.shape[1]
    blocks = lax.axis_size("rows")
    me = lax.axis_index("rows")
    tile = flat // blocks
    wide = tile // depth

    def fetch(p):
        columns = pl.ds(pl.multiple_of((me ^ p) * tile, tile), tile)
        return pltpu.make_async_copy(n_ref.at[:, columns], held_ref.at[p], sems.at[p])

    for p in range(blocks):
        fetch(p).start()
    low_a = a_ref[...]
    c = c_ref[...]
    acc_ref[...] = jnp.zeros_like(acc_ref)
    grad_c = jnp.zeros((depth, rank), F32)
    for p in range(blocks):
        owner = me ^ p
        level = p.bit_length()
        first = (p - (1 << level >> 1)) * wide if p else 0
        low_b = b_refs[level][first : first + wide].astype(F32)
        scaled = (low_b[:, None, :] * c[None]).astype(BF16).reshape(tile, rank)
        log_rate = lax.dot_general(
            low_a, scaled, (((1,), (1,)), ((), ())), preferred_element_type=F32
        )
        fetch(p).wait()
        residual = (jnp.exp(log_rate) - held_ref[p].astype(F32)).astype(BF16)
        mixed = lax.dot_general(
            residual, low_a, (((0,), (0,)), ((), ())), preferred_element_type=F32
        ).reshape(wide, depth, rank)
        grad_b = jnp.sum(mixed * c[None], axis=1).astype(BF16)
        if last:
            xb_ref[owner, :wide] = grad_b
        else:
            xb_ref[p * wide : (p + 1) * wide] = grad_b
        grad_c = grad_c + jnp.sum(mixed * low_b[:, None, :], axis=0)
        acc_ref[...] += jnp.dot(residual, scaled, preferred_element_type=F32)
    parts, rows = xa_ref.shape[0], low_a.shape[0] // xa_ref.shape[0]
    low_c = grad_c.astype(BF16)
    xa_ref[:, :rows] = acc_ref[...].astype(BF16).reshape(parts, rows, rank)
    if last:
        xb_ref[:, wide:] = jnp.broadcast_to(low_c[None], (blocks, depth, rank))
    else:
        xa_ref[:, rows:] = jnp.broadcast_to(low_c[None], (parts, depth, rank))


def grads(counts, low_a, b_parts, c, last):
    rows, flat = counts.shape
    depth, rank = c.shape
    wide = flat // depth
    blocks, parts = lax.axis_size("rows"), lax.axis_size("cols")
    whole = pl.BlockSpec(memory_space=pltpu.VMEM)
    shape_a = (parts, rows // parts + (0 if last else depth), rank)
    shape_b = (blocks, wide // blocks + depth, rank) if last else (wide, rank)
    return pl.pallas_call(
        functools.partial(grads_body, last),
        in_specs=[pl.BlockSpec(memory_space=pltpu.HBM)] + [whole] * (2 + len(b_parts)),
        out_specs=[whole] * 2,
        out_shape=[
            jax.ShapeDtypeStruct(shape_a, BF16),
            jax.ShapeDtypeStruct(shape_b, BF16),
        ],
        scratch_shapes=[
            pltpu.VMEM((rows, rank), F32),
            pltpu.VMEM((blocks, rows, flat // blocks), BF16),
            pltpu.SemaphoreType.DMA((blocks,)),
        ],
        compiler_params=pltpu.CompilerParams(vmem_limit_bytes=32 << 20),
        cost_estimate=pl.CostEstimate(
            flops=6 * rows * flat * rank,
            transcendentals=rows * flat,
            bytes_accessed=2 * rows * flat,
        ),
    )(counts, low_a, *b_parts, c)


def swap(piece, bit):
    n = lax.axis_size("rows")
    return lax.ppermute(piece, "rows", [(i, i ^ bit) for i in range(n)])


def gather_cols(piece):
    n = lax.axis_size("cols")
    out = lax.all_to_all(jnp.broadcast_to(piece[None], (n, *piece.shape)), "cols", 0, 0)
    return out.reshape(n * piece.shape[0], piece.shape[1])


def exchange(pieces, axis):
    return jnp.sum(lax.all_to_all(pieces, axis, 0, 0).astype(F32), axis=0)


def gather_rows(piece, extra=None):
    held = [piece]
    bit = 1
    while bit < lax.axis_size("rows"):
        held.append(swap(jnp.concatenate(held), bit))
        if extra is not None:
            low = extra.astype(BF16)
            extra = low.astype(F32) + swap(low, bit).astype(F32)
        bit *= 2
    return held, extra


def scatter_rows(whole):
    bit = lax.axis_size("rows") // 2
    while bit:
        half = whole.shape[0] // 2
        got = swap(whole[half:], bit)
        whole = whole[:half].astype(F32) + got.astype(F32)
        if bit > 1:
            whole = whole.astype(BF16)
        bit //= 2
    return whole


def local(counts, start_a, start_b, start_c):
    rows_here, flat_width = counts.shape
    depth = start_c.shape[0]
    cols_here = flat_width // depth
    total_i = rows_here * lax.axis_size("rows")
    total_j = cols_here * lax.axis_size("cols")
    rate_a = 0.3 / math.sqrt(total_j * depth)
    rate_b = 0.3 / math.sqrt(total_i * depth)
    rate_c = 0.3 / math.sqrt(total_i * total_j)
    counts = pltpu.with_memory_space_constraint(counts, pltpu.HBM)
    local_a, local_b, shared_c = (start_a, start_b, start_c)
    part_c = None
    for iteration in range(ITERS):
        last = iteration == ITERS - 1
        low_a = gather_cols(local_a.astype(BF16))
        b_parts, summed_c = gather_rows(local_b.astype(BF16), part_c)
        if summed_c is not None:
            shared_c = shared_c - rate_c * summed_c
        pieces_a, pieces_b = grads(counts, low_a, b_parts, shared_c, last)
        rows_a, rows_b = local_a.shape[0], local_b.shape[0]
        if last:
            total_b = exchange(pieces_b, "rows")
            low_c = jnp.broadcast_to(
                total_b[None, rows_b:].astype(BF16), (pieces_a.shape[0], depth, start_c.shape[1])
            )
            total_a = exchange(jnp.concatenate([pieces_a, low_c], axis=1), "cols")
            local_b = local_b - rate_b * total_b[:rows_b]
            shared_c = shared_c - rate_c * total_a[rows_a:]
        else:
            total_a = exchange(pieces_a, "cols")
            local_b = local_b - rate_b * scatter_rows(pieces_b)
            part_c = total_a[rows_a:]
        local_a = local_a - rate_a * total_a[:rows_a]
    return (local_a, local_b, shared_c)


def solution(mesh):
    placed = (P("rows", "cols"), P(("rows", "cols"), None), P(("cols", "rows"), None), P())
    return jax.shard_map(
        local,
        mesh=mesh,
        in_specs=placed,
        out_specs=(P(("rows", "cols"), None), P(("cols", "rows"), None), P()),
        check_vma=False,
    )
```

```python
import functools
import math

import jax
import jax.numpy as jnp
from jax import lax
from jax.experimental import pallas as pl
from jax.experimental.pallas import tpu as pltpu
from jax.sharding import PartitionSpec as P

ITERS = 2
BF16 = jnp.bfloat16
F32 = jnp.float32
IN_FLIGHT = 3
WHOLE = pl.BlockSpec(memory_space=pltpu.VMEM)


def prepare_body(a_ref, b_ref, c_ref, copies_ref, low_b_ref, held_c_ref, a_buf, b_buf, sems):
    into = ((a_ref, a_buf), (b_ref, b_buf), (c_ref, held_c_ref))
    moves = [pltpu.make_async_copy(src, dst, sems.at[k]) for k, (src, dst) in enumerate(into)]
    for move in moves:
        move.start()
    moves[1].wait()
    low_b_ref[...] = b_buf[...].astype(BF16)
    moves[0].wait()
    copies_ref[...] = jnp.broadcast_to(a_buf[...].astype(BF16)[None], copies_ref.shape)
    moves[2].wait()


def prepare(a, b, c):
    operands = [pltpu.with_memory_space_constraint(x, pltpu.HBM) for x in (a, b, c)]
    return pl.pallas_call(
        prepare_body,
        in_specs=[pl.BlockSpec(memory_space=pltpu.HBM)] * 3,
        out_specs=[WHOLE] * 3,
        out_shape=[
            jax.ShapeDtypeStruct((lax.axis_size("cols"), *a.shape), BF16),
            jax.ShapeDtypeStruct(b.shape, BF16),
            jax.ShapeDtypeStruct(c.shape, F32),
        ],
        scratch_shapes=[
            pltpu.VMEM(a.shape, F32),
            pltpu.VMEM(b.shape, F32),
            pltpu.SemaphoreType.DMA((3,)),
        ],
        compiler_params=pltpu.CompilerParams(vmem_limit_bytes=2 << 20),
    )(*operands)


def visit_blocks(order, n_ref, held_ref, sems, low_a, b_of, c, put_b, acc_ref, grad_c):
    depth, rank = c.shape
    blocks = lax.axis_size("rows")
    me = lax.axis_index("rows")
    tile = n_ref.shape[1] // blocks
    wide = tile // depth

    def fetch(k):
        columns = pl.ds(pl.multiple_of((me ^ order[k]) * tile, tile), tile)
        return pltpu.make_async_copy(n_ref.at[:, columns], held_ref.at[k], sems.at[k])

    for k in range(min(IN_FLIGHT, len(order))):
        fetch(k).start()
    for k, p in enumerate(order):
        low_b = b_of(p).astype(F32)
        scaled = (low_b[:, None, :] * c[None]).astype(BF16).reshape(tile, rank)
        log_rate = lax.dot_general(
            low_a, scaled, (((1,), (1,)), ((), ())), preferred_element_type=F32
        )
        fetch(k).wait()
        if k + IN_FLIGHT < len(order):
            fetch(k + IN_FLIGHT).start()
        residual = (jnp.exp(log_rate) - held_ref[k].astype(F32)).astype(BF16)
        mixed = lax.dot_general(
            residual, low_a, (((0,), (0,)), ((), ())), preferred_element_type=F32
        ).reshape(wide, depth, rank)
        put_b(p, jnp.sum(mixed * c[None], axis=1).astype(BF16))
        grad_c = grad_c + jnp.sum(mixed * low_b[:, None, :], axis=0)
        acc_ref[...] += jnp.dot(residual, scaled, preferred_element_type=F32)
    return grad_c


def parts_of(b_refs, wide):
    def b_of(p):
        level = p.bit_length()
        start = (p - (1 << level >> 1)) * wide
        return b_refs[level][start : start + wide]

    return b_of


def first_body(n_ref, a_ref, *refs):
    b_refs, (c_ref, xa_ref, near_ref, far_ref, acc_ref, held_ref, sems) = refs[:-7], refs[-7:]
    blocks = lax.axis_size("rows")
    half = near_ref.shape[0]
    wide = 2 * half // blocks

    def put_b(p, value):
        at = p * wide % half
        (near_ref if p < blocks // 2 else far_ref)[at : at + wide] = value

    low_a = a_ref[...].reshape(acc_ref.shape)
    acc_ref[...] = jnp.zeros_like(acc_ref)
    b_of = parts_of(b_refs, wide)
    grad_c = jnp.zeros(c_ref.shape, F32)
    grad_c = visit_blocks(
        range(blocks), n_ref, held_ref, sems, low_a, b_of, c_ref[...], put_b, acc_ref, grad_c
    )
    xa_ref[...] = acc_ref[...].astype(BF16).reshape(xa_ref.shape)
    far_ref[half:] = grad_c.astype(BF16)


def last_body(rate_c, n_ref, a_ref, *refs):
    b_refs, (c_ref, xa_ref, xb_ref, new_c_ref, acc_ref, held_ref, sems) = refs[:-7], refs[-7:]
    depth, rank = c_ref.shape
    blocks = lax.axis_size("rows")
    me = lax.axis_index("rows")
    wide = xb_ref.shape[1] - depth
    parts, rows, _ = xa_ref.shape

    def put_b(p, value):
        xb_ref[me ^ p, :wide] = value

    acc_ref[...] = jnp.zeros_like(acc_ref)
    low_a = a_ref[:, :rows].reshape(acc_ref.shape)
    c = c_ref[...] - rate_c * jnp.sum(a_ref[:, rows:].astype(F32), axis=0)
    new_c_ref[...] = c
    b_of = parts_of(b_refs, wide)
    grad_c = jnp.zeros(c.shape, F32)
    grad_c = visit_blocks(
        range(blocks), n_ref, held_ref, sems, low_a, b_of, c, put_b, acc_ref, grad_c
    )
    xa_ref[...] = acc_ref[...].astype(BF16).reshape(xa_ref.shape)
    xb_ref[:, wide:] = jnp.broadcast_to(grad_c.astype(BF16)[None], (blocks, depth, rank))


def call(body, counts, operands, outs):
    rows, flat = counts.shape
    rank = operands[0].shape[-1]
    blocks = lax.axis_size("rows")
    return pl.pallas_call(
        body,
        in_specs=[pl.BlockSpec(memory_space=pltpu.HBM)] + [WHOLE] * len(operands),
        out_specs=[WHOLE] * len(outs),
        out_shape=[jax.ShapeDtypeStruct(shape, dtype) for shape, dtype in outs],
        scratch_shapes=[
            pltpu.VMEM((rows, rank), F32),
            pltpu.VMEM((blocks, rows, flat // blocks), BF16),
            pltpu.SemaphoreType.DMA((blocks,)),
        ],
        compiler_params=pltpu.CompilerParams(vmem_limit_bytes=32 << 20),
        cost_estimate=pl.CostEstimate(
            flops=6 * rows * flat * rank,
            transcendentals=rows * flat,
            bytes_accessed=2 * rows * flat,
        ),
    )(counts, *operands)


def swap(piece, bit):
    n = lax.axis_size("rows")
    return lax.ppermute(piece, "rows", [(i, i ^ bit) for i in range(n)])


def copies_of(piece):
    return jnp.broadcast_to(piece[None], (lax.axis_size("cols"), *piece.shape))


def total(pieces):
    return jnp.sum(pieces.astype(F32), axis=0)


def gather_rows(piece):
    held = [piece]
    bit = 1
    while bit < lax.axis_size("rows"):
        held.append(swap(jnp.concatenate(held), bit))
        bit *= 2
    return held


def reduce_rows(near, far):
    bit = lax.axis_size("rows") // 2
    half = near.shape[0]
    got = swap(far, bit).astype(F32)
    kept = near.astype(F32) + got[:half]
    extra = far[half:].astype(F32) + got[half:]
    while bit > 1:
        bit //= 2
        kept, extra = kept.astype(BF16), extra.astype(BF16)
        half //= 2
        got_extra = swap(extra, bit)
        kept = kept[:half].astype(F32) + swap(kept[half:], bit).astype(F32)
        extra = extra.astype(F32) + got_extra.astype(F32)
    return kept, extra.astype(BF16)


def local(counts, start_a, start_b, start_c):
    rows_here, flat_width = counts.shape
    depth, rank = start_c.shape
    cols_here = flat_width // depth
    n_rows, n_cols = lax.axis_size("rows"), lax.axis_size("cols")
    total_i = rows_here * n_rows
    total_j = cols_here * n_cols
    rate_a = 0.3 / math.sqrt(total_j * depth)
    rate_b = 0.3 / math.sqrt(total_i * depth)
    rate_c = 0.3 / math.sqrt(total_i * total_j)
    counts = pltpu.with_memory_space_constraint(counts, pltpu.HBM)
    local_a, local_b = start_a, start_b
    rows_a, rows_b = start_a.shape[0], start_b.shape[0]
    shape_a = (n_cols, rows_a, rank)
    copies, low_b, c = prepare(start_a, start_b, start_c)
    for _ in range(ITERS - 1):
        got = lax.all_to_all(copies, "cols", 0, 0)
        assert got.shape == shape_a
        half = cols_here // 2
        pieces_a, near_b, far_b = call(
            first_body, counts, [got, *gather_rows(low_b), c],
            [(shape_a, BF16), ((half, rank), BF16), ((half + depth, rank), BF16)],
        )
        part_b, low_c = reduce_rows(near_b, far_b)
        local_b = local_b - rate_b * part_b
        low_b = local_b.astype(BF16)
        local_a = local_a - rate_a * total(lax.all_to_all(pieces_a, "cols", 0, 0))
        copies = copies_of(jnp.concatenate([local_a.astype(BF16), low_c]))
        copies, low_b = lax.optimization_barrier((copies, low_b))
    got = lax.all_to_all(copies, "cols", 0, 0)
    b_parts = gather_rows(low_b)
    pieces_a, pieces_b, c = call(
        functools.partial(last_body, rate_c), counts, [got, *b_parts, c],
        [(shape_a, BF16), ((n_rows, rows_b + depth, rank), BF16), (c.shape, F32)],
    )
    part_b = total(lax.all_to_all(pieces_b, "rows", 0, 0))
    part_c = copies_of(part_b[rows_b:].astype(BF16))
    sums = total(lax.all_to_all(jnp.concatenate([pieces_a, part_c], axis=1), "cols", 0, 0))
    return (
        local_a - rate_a * sums[:rows_a],
        local_b - rate_b * part_b[:rows_b],
        c - rate_c * sums[rows_a:],
    )


def solution(mesh):
    placed = (P("rows", "cols"), P(("rows", "cols"), None), P(("cols", "rows"), None), P())
    return jax.shard_map(
        local,
        mesh=mesh,
        in_specs=placed,
        out_specs=(P(("rows", "cols"), None), P(("cols", "rows"), None), P()),
        check_vma=False,
    )
```

```python
import functools
import math

import jax
import jax.numpy as jnp
from jax import lax
from jax.experimental import pallas as pl
from jax.experimental.pallas import tpu as pltpu
from jax.sharding import PartitionSpec as P

ITERS = 2
BF16 = jnp.bfloat16
F32 = jnp.float32
WAITS = {0: (0,), 1: (1, 2), 4: (3,)}
JOIN_WEIGHT = 3_000_000_000
WHOLE = pl.BlockSpec(memory_space=pltpu.VMEM)


def prepare_body(a_ref, b_ref, c_ref, copies_ref, low_b_ref, held_c_ref, a_buf, b_buf, sems):
    into = ((a_ref, a_buf), (b_ref, b_buf), (c_ref, held_c_ref))
    moves = [pltpu.make_async_copy(src, dst, sems.at[k]) for k, (src, dst) in enumerate(into)]
    for move in moves:
        move.start()
    moves[1].wait()
    low_b_ref[...] = b_buf[...].astype(BF16)
    moves[0].wait()
    copies_ref[...] = jnp.broadcast_to(a_buf[...].astype(BF16)[None], copies_ref.shape)
    moves[2].wait()


def prepare(a, b, c):
    operands = [pltpu.with_memory_space_constraint(x, pltpu.HBM) for x in (a, b, c)]
    return pl.pallas_call(
        prepare_body,
        in_specs=[pl.BlockSpec(memory_space=pltpu.HBM)] * 3,
        out_specs=[WHOLE] * 3,
        out_shape=[
            jax.ShapeDtypeStruct((lax.axis_size("cols"), *a.shape), BF16),
            jax.ShapeDtypeStruct(b.shape, BF16),
            jax.ShapeDtypeStruct(c.shape, F32),
        ],
        scratch_shapes=[
            pltpu.VMEM(a.shape, F32),
            pltpu.VMEM(b.shape, F32),
            pltpu.SemaphoreType.DMA((3,)),
        ],
        compiler_params=pltpu.CompilerParams(vmem_limit_bytes=2 << 20),
    )(*operands)


def update_body(rate_a, rate_b, got_ref, a_ref, sum_b_ref, b_ref, low_c_ref, *outs):
    copies_ref, low_b_ref, new_a_ref, new_b_ref = outs
    new_b = b_ref[...] - rate_b * sum_b_ref[...]
    new_b_ref[...] = new_b
    low_b_ref[...] = new_b.astype(BF16)
    new_a = a_ref[...] - rate_a * total(got_ref[...])
    new_a_ref[...] = new_a
    parts, height, rank = copies_ref.shape
    rows = new_a.shape[0]
    copies_ref[:, :rows] = jnp.broadcast_to(new_a.astype(BF16)[None], (parts, rows, rank))
    copies_ref[:, rows:] = jnp.broadcast_to(low_c_ref[...][None], (parts, height - rows, rank))


def update(got, a, sum_b, b, low_c, rate_a, rate_b):
    parts, rows, rank = got.shape
    return pl.pallas_call(
        functools.partial(update_body, rate_a, rate_b),
        in_specs=[WHOLE] * 5,
        out_specs=[WHOLE] * 4,
        out_shape=[
            jax.ShapeDtypeStruct((parts, rows + low_c.shape[0], rank), BF16),
            jax.ShapeDtypeStruct(b.shape, BF16),
            jax.ShapeDtypeStruct(a.shape, F32),
            jax.ShapeDtypeStruct(b.shape, F32),
        ],
        compiler_params=pltpu.CompilerParams(vmem_limit_bytes=2 << 20),
    )(got, a, sum_b, b, low_c)


def visit_blocks(n_ref, held_ref, sems, low_a, b_of, c, put_b, acc_ref, grad_c):
    depth, rank = c.shape
    blocks = lax.axis_size("rows")
    me = lax.axis_index("rows")
    tile = n_ref.shape[1] // blocks
    wide = tile // depth

    def fetch(level):
        count = max(1 << level >> 1, 1)
        first = (me ^ (1 << level >> 1)) // count * count
        columns = pl.ds(pl.multiple_of(first * tile, tile), count * tile)
        return pltpu.make_async_copy(n_ref.at[:, columns], held_ref.at[:, columns], sems.at[level])

    levels = blocks.bit_length()
    for level in range(levels):
        fetch(level).start()
    for p in range(blocks):
        columns = pl.ds(pl.multiple_of((me ^ p) * tile, tile), tile)
        low_b = b_of(p).astype(F32)
        scaled = (low_b[:, None, :] * c[None]).astype(BF16).reshape(tile, rank)
        log_rate = lax.dot_general(
            low_a, scaled, (((1,), (1,)), ((), ())), preferred_element_type=F32
        )
        for level in WAITS.get(p, ()):
            fetch(level).wait()
        residual = (jnp.exp(log_rate) - held_ref[:, columns].astype(F32)).astype(BF16)
        mixed = lax.dot_general(
            residual, low_a, (((0,), (0,)), ((), ())), preferred_element_type=F32
        ).reshape(wide, depth, rank)
        put_b(p, jnp.sum(mixed * c[None], axis=1).astype(BF16))
        grad_c = grad_c + jnp.sum(mixed * low_b[:, None, :], axis=0)
        acc_ref[...] += jnp.dot(residual, scaled, preferred_element_type=F32)
    return grad_c


def parts_of(b_refs, wide):
    def b_of(x):
        steps = len(b_refs) - 1
        p = sum((x >> k & 1) << (steps - 1 - k) for k in range(steps))
        step = p.bit_length()
        start = (p - (1 << step >> 1)) * wide
        return b_refs[step][start : start + wide]

    return b_of


def first_body(n_ref, a_ref, *refs):
    b_refs, (c_ref, xa_ref, near_ref, far_ref, acc_ref, held_ref, sems) = refs[:-7], refs[-7:]
    blocks = lax.axis_size("rows")
    half = near_ref.shape[0]
    wide = 2 * half // blocks

    def put_b(p, value):
        at = p * wide % half
        (near_ref if p < blocks // 2 else far_ref)[at : at + wide] = value

    low_a = a_ref[...].reshape(acc_ref.shape)
    acc_ref[...] = jnp.zeros_like(acc_ref)
    b_of = parts_of(b_refs, wide)
    grad_c = jnp.zeros(c_ref.shape, F32)
    grad_c = visit_blocks(
        n_ref, held_ref, sems, low_a, b_of, c_ref[...], put_b, acc_ref, grad_c
    )
    xa_ref[...] = acc_ref[...].astype(BF16).reshape(xa_ref.shape)
    far_ref[half:] = grad_c.astype(BF16)


def last_body(rate_c, n_ref, a_ref, *refs):
    b_refs, (c_ref, xa_ref, xb_ref, new_c_ref, acc_ref, held_ref, sems) = refs[:-7], refs[-7:]
    depth, rank = c_ref.shape
    blocks = lax.axis_size("rows")
    me = lax.axis_index("rows")
    wide = xb_ref.shape[1] - depth
    parts, rows, _ = xa_ref.shape

    def put_b(p, value):
        xb_ref[me ^ p, :wide] = value

    acc_ref[...] = jnp.zeros_like(acc_ref)
    low_a = a_ref[:, :rows].reshape(acc_ref.shape)
    c = c_ref[...] - rate_c * jnp.sum(a_ref[:, rows:].astype(F32), axis=0)
    new_c_ref[...] = c
    b_of = parts_of(b_refs, wide)
    grad_c = jnp.zeros(c.shape, F32)
    grad_c = visit_blocks(
        n_ref, held_ref, sems, low_a, b_of, c, put_b, acc_ref, grad_c
    )
    xa_ref[...] = acc_ref[...].astype(BF16).reshape(xa_ref.shape)
    xb_ref[:, wide:] = jnp.broadcast_to(grad_c.astype(BF16)[None], (blocks, depth, rank))


def call(body, counts, operands, outs):
    rows, flat = counts.shape
    rank = operands[0].shape[-1]
    return pl.pallas_call(
        body,
        in_specs=[pl.BlockSpec(memory_space=pltpu.HBM)] + [WHOLE] * len(operands),
        out_specs=[WHOLE] * len(outs),
        out_shape=[jax.ShapeDtypeStruct(shape, dtype) for shape, dtype in outs],
        scratch_shapes=[
            pltpu.VMEM((rows, rank), F32),
            pltpu.VMEM((rows, flat), BF16),
            pltpu.SemaphoreType.DMA((lax.axis_size("rows").bit_length(),)),
        ],
        compiler_params=pltpu.CompilerParams(vmem_limit_bytes=32 << 20),
        cost_estimate=pl.CostEstimate(
            flops=6 * rows * flat * rank,
            transcendentals=rows * flat,
            bytes_accessed=2 * rows * flat,
        ),
    )(counts, *operands)


def swap(piece, bit):
    n = lax.axis_size("rows")
    return lax.ppermute(piece, "rows", [(i, i ^ bit) for i in range(n)])


def copies_of(piece):
    return jnp.broadcast_to(piece[None], (lax.axis_size("cols"), *piece.shape))


def total(pieces):
    return jnp.sum(pieces.astype(F32), axis=0)


def join_body(*refs):
    *pieces, out_ref = refs
    at = 0
    for piece in pieces:
        out_ref[at : at + piece.shape[0]] = piece[...]
        at += piece.shape[0]


def join(pieces, weight):
    rows = sum(piece.shape[0] for piece in pieces)
    return pl.pallas_call(
        join_body,
        in_specs=[WHOLE] * len(pieces),
        out_specs=WHOLE,
        out_shape=jax.ShapeDtypeStruct((rows, pieces[0].shape[1]), pieces[0].dtype),
        compiler_params=pltpu.CompilerParams(vmem_limit_bytes=2 << 20),
        cost_estimate=pl.CostEstimate(flops=weight, transcendentals=0, bytes_accessed=0),
    )(*pieces)


def gather_rows(piece, weight=0):
    held = [piece]
    bit = lax.axis_size("rows") // 2
    while bit:
        whole = join(held, weight) if weight and bit == 1 else jnp.concatenate(held)
        held.append(swap(whole, bit))
        bit //= 2
    return held


def reduce_rows(near, far):
    bit = lax.axis_size("rows") // 2
    half = near.shape[0]
    got = swap(far, bit).astype(F32)
    kept = near.astype(F32) + got[:half]
    extra = far[half:].astype(F32) + got[half:]
    while bit > 1:
        bit //= 2
        kept, extra = kept.astype(BF16), extra.astype(BF16)
        half //= 2
        got_extra = swap(extra, bit)
        kept = kept[:half].astype(F32) + swap(kept[half:], bit).astype(F32)
        extra = extra.astype(F32) + got_extra.astype(F32)
    return kept, extra.astype(BF16)


def local(counts, start_a, start_b, start_c):
    rows_here, flat_width = counts.shape
    depth, rank = start_c.shape
    cols_here = flat_width // depth
    n_rows, n_cols = lax.axis_size("rows"), lax.axis_size("cols")
    total_i = rows_here * n_rows
    total_j = cols_here * n_cols
    rate_a = 0.3 / math.sqrt(total_j * depth)
    rate_b = 0.3 / math.sqrt(total_i * depth)
    rate_c = 0.3 / math.sqrt(total_i * total_j)
    counts = pltpu.with_memory_space_constraint(counts, pltpu.HBM)
    local_a, local_b = start_a, start_b
    rows_a, rows_b = start_a.shape[0], start_b.shape[0]
    shape_a = (n_cols, rows_a, rank)
    copies, low_b, c = prepare(start_a, start_b, start_c)
    for _ in range(ITERS - 1):
        got = lax.all_to_all(copies, "cols", 0, 0)
        assert got.shape == shape_a
        half = cols_here // 2
        pieces_a, near_b, far_b = call(
            first_body, counts, [got, *gather_rows(low_b), c],
            [(shape_a, BF16), ((half, rank), BF16), ((half + depth, rank), BF16)],
        )
        part_b, low_c = reduce_rows(near_b, far_b)
        got = lax.all_to_all(pieces_a, "cols", 0, 0)
        copies, low_b, local_a, local_b = update(
            got, local_a, part_b, local_b, low_c, rate_a, rate_b
        )
    got = lax.all_to_all(copies, "cols", 0, 0)
    b_parts = gather_rows(low_b, JOIN_WEIGHT)
    pieces_a, pieces_b, c = call(
        functools.partial(last_body, rate_c), counts, [got, *b_parts, c],
        [(shape_a, BF16), ((n_rows, rows_b + depth, rank), BF16), (c.shape, F32)],
    )
    part_b = total(lax.all_to_all(pieces_b, "rows", 0, 0))
    part_c = copies_of(part_b[rows_b:].astype(BF16))
    sums = lax.all_to_all(jnp.concatenate([pieces_a, part_c], axis=1), "cols", 0, 0)
    sums, part_b = lax.optimization_barrier((sums, part_b))
    sums = total(sums)
    return (
        local_a - rate_a * sums[:rows_a],
        local_b - rate_b * part_b[:rows_b],
        c - rate_c * sums[rows_a:],
    )


def solution(mesh):
    placed = (P("rows", "cols"), P(("rows", "cols"), None), P(("cols", "rows"), None), P())
    return jax.shard_map(
        local,
        mesh=mesh,
        in_specs=placed,
        out_specs=(P(("rows", "cols"), None), P(("cols", "rows"), None), P()),
        check_vma=False,
    )
```

```python
import functools
import math

import jax
import jax.numpy as jnp
from jax import lax
from jax.experimental import pallas as pl
from jax.experimental.pallas import tpu as pltpu
from jax.sharding import PartitionSpec as P

ITERS = 2
BF16 = jnp.bfloat16
F32 = jnp.float32
WAITS = {0: (0,), 1: (1, 2), 4: (3,)}
JOIN_WEIGHT = 3_000_000_000
WHOLE = pl.BlockSpec(memory_space=pltpu.VMEM)


def prepare_body(a_ref, b_ref, c_ref, copies_ref, low_b_ref, held_c_ref, a_buf, b_buf, sems):
    into = ((a_ref, a_buf), (b_ref, b_buf), (c_ref, held_c_ref))
    moves = [pltpu.make_async_copy(src, dst, sems.at[k]) for k, (src, dst) in enumerate(into)]
    for move in moves:
        move.start()
    moves[1].wait()
    low_b_ref[...] = b_buf[...].astype(BF16)
    moves[0].wait()
    copies_ref[...] = jnp.broadcast_to(a_buf[...].astype(BF16)[None], copies_ref.shape)
    moves[2].wait()


def prepare(a, b, c):
    operands = [pltpu.with_memory_space_constraint(x, pltpu.HBM) for x in (a, b, c)]
    return pl.pallas_call(
        prepare_body,
        in_specs=[pl.BlockSpec(memory_space=pltpu.HBM)] * 3,
        out_specs=[WHOLE] * 3,
        out_shape=[
            jax.ShapeDtypeStruct((lax.axis_size("cols"), *a.shape), BF16),
            jax.ShapeDtypeStruct(b.shape, BF16),
            jax.ShapeDtypeStruct(c.shape, F32),
        ],
        scratch_shapes=[
            pltpu.VMEM(a.shape, F32),
            pltpu.VMEM(b.shape, F32),
            pltpu.SemaphoreType.DMA((3,)),
        ],
        compiler_params=pltpu.CompilerParams(vmem_limit_bytes=2 << 20),
    )(*operands)


def update_body(rate_a, rate_b, got_ref, a_ref, sum_b_ref, b_ref, low_c_ref, *outs):
    copies_ref, low_b_ref, new_a_ref, new_b_ref = outs
    new_b = b_ref[...] - rate_b * sum_b_ref[...]
    new_b_ref[...] = new_b
    low_b_ref[...] = new_b.astype(BF16)
    new_a = a_ref[...] - rate_a * total(got_ref[...])
    new_a_ref[...] = new_a
    parts, height, rank = copies_ref.shape
    rows = new_a.shape[0]
    copies_ref[:, :rows] = jnp.broadcast_to(new_a.astype(BF16)[None], (parts, rows, rank))
    copies_ref[:, rows:] = jnp.broadcast_to(low_c_ref[...][None], (parts, height - rows, rank))


def update(got, a, sum_b, b, low_c, rate_a, rate_b):
    parts, rows, rank = got.shape
    return pl.pallas_call(
        functools.partial(update_body, rate_a, rate_b),
        in_specs=[WHOLE] * 5,
        out_specs=[WHOLE] * 4,
        out_shape=[
            jax.ShapeDtypeStruct((parts, rows + low_c.shape[0], rank), BF16),
            jax.ShapeDtypeStruct(b.shape, BF16),
            jax.ShapeDtypeStruct(a.shape, F32),
            jax.ShapeDtypeStruct(b.shape, F32),
        ],
        compiler_params=pltpu.CompilerParams(vmem_limit_bytes=2 << 20),
    )(got, a, sum_b, b, low_c)


def visit_blocks(n_ref, held_ref, sems, low_a, b_of, c, put_b, acc_ref, grad_c):
    depth, rank = c.shape
    blocks = lax.axis_size("rows")
    me = lax.axis_index("rows")
    tile = n_ref.shape[1] // blocks
    wide = tile // depth

    def fetch(level):
        count = max(1 << level >> 1, 1)
        first = (me ^ (1 << level >> 1)) // count * count
        columns = pl.ds(pl.multiple_of(first * tile, tile), count * tile)
        return pltpu.make_async_copy(n_ref.at[:, columns], held_ref.at[:, columns], sems.at[level])

    levels = blocks.bit_length()
    for level in range(levels):
        fetch(level).start()
    for p in range(blocks):
        columns = pl.ds(pl.multiple_of((me ^ p) * tile, tile), tile)
        low_b = b_of(p).astype(F32)
        scaled = (low_b[:, None, :] * c[None]).astype(BF16).reshape(tile, rank)
        log_rate = lax.dot_general(
            low_a, scaled, (((1,), (1,)), ((), ())), preferred_element_type=F32
        )
        for level in WAITS.get(p, ()):
            fetch(level).wait()
        residual = (jnp.exp(log_rate) - held_ref[:, columns].astype(F32)).astype(BF16)
        mixed = lax.dot_general(
            residual, low_a, (((0,), (0,)), ((), ())), preferred_element_type=F32
        ).reshape(wide, depth, rank)
        put_b(p, jnp.sum(mixed * c[None], axis=1).astype(BF16))
        grad_c = grad_c + jnp.sum(mixed * low_b[:, None, :], axis=0)
        acc_ref[...] += jnp.dot(residual, scaled, preferred_element_type=F32)
    return grad_c


def parts_of(b_refs, wide):
    def b_of(x):
        steps = len(b_refs) - 1
        p = sum((x >> k & 1) << (steps - 1 - k) for k in range(steps))
        step = p.bit_length()
        start = (p - (1 << step >> 1)) * wide
        return b_refs[step][start : start + wide]

    return b_of


def first_body(n_ref, a_ref, *refs):
    b_refs, (c_ref, xa_ref, near_ref, far_ref, acc_ref, held_ref, sems) = refs[:-7], refs[-7:]
    blocks = lax.axis_size("rows")
    half = near_ref.shape[0]
    wide = 2 * half // blocks

    def put_b(p, value):
        at = p * wide % half
        (near_ref if p < blocks // 2 else far_ref)[at : at + wide] = value

    low_a = a_ref[...].reshape(acc_ref.shape)
    acc_ref[...] = jnp.zeros_like(acc_ref)
    b_of = parts_of(b_refs, wide)
    grad_c = jnp.zeros(c_ref.shape, F32)
    grad_c = visit_blocks(
        n_ref, held_ref, sems, low_a, b_of, c_ref[...], put_b, acc_ref, grad_c
    )
    xa_ref[...] = acc_ref[...].astype(BF16).reshape(xa_ref.shape)
    far_ref[half:] = grad_c.astype(BF16)


def last_body(rate_c, n_ref, a_ref, *refs):
    b_refs, rest = refs[:-8], refs[-8:]
    c_ref, own_ref, other_ref, xb_ref, new_c_ref, acc_ref, held_ref, sems = rest
    depth, rank = c_ref.shape
    blocks = lax.axis_size("rows")
    me = lax.axis_index("rows")
    wide = xb_ref.shape[1] - depth
    chips, rows, _ = own_ref.shape
    core = lax.axis_index("cols") % 2

    def put_b(p, value):
        xb_ref[me ^ p, :wide] = value

    acc_ref[...] = jnp.zeros_like(acc_ref)
    low_a = a_ref[:, :rows].reshape(acc_ref.shape)
    c = c_ref[...] - rate_c * jnp.sum(a_ref[:, rows:].astype(F32), axis=0)
    new_c_ref[...] = c
    b_of = parts_of(b_refs, wide)
    grad_c = jnp.zeros(c.shape, F32)
    grad_c = visit_blocks(
        n_ref, held_ref, sems, low_a, b_of, c, put_b, acc_ref, grad_c
    )
    for chip in range(chips):
        for piece_ref, which in ((own_ref, core), (other_ref, 1 - core)):
            at = pl.multiple_of((2 * chip + which) * rows, rows)
            piece_ref[chip] = acc_ref[pl.ds(at, rows)].astype(BF16)
    xb_ref[:, wide:] = jnp.broadcast_to(grad_c.astype(BF16)[None], (blocks, depth, rank))


def call(body, counts, operands, outs):
    rows, flat = counts.shape
    rank = operands[0].shape[-1]
    return pl.pallas_call(
        body,
        in_specs=[pl.BlockSpec(memory_space=pltpu.HBM)] + [WHOLE] * len(operands),
        out_specs=[WHOLE] * len(outs),
        out_shape=[jax.ShapeDtypeStruct(shape, dtype) for shape, dtype in outs],
        scratch_shapes=[
            pltpu.VMEM((rows, rank), F32),
            pltpu.VMEM((rows, flat), BF16),
            pltpu.SemaphoreType.DMA((lax.axis_size("rows").bit_length(),)),
        ],
        compiler_params=pltpu.CompilerParams(vmem_limit_bytes=32 << 20),
        cost_estimate=pl.CostEstimate(
            flops=6 * rows * flat * rank,
            transcendentals=rows * flat,
            bytes_accessed=2 * rows * flat,
        ),
    )(counts, *operands)


def swap(piece, bit):
    n = lax.axis_size("rows")
    return lax.ppermute(piece, "rows", [(i, i ^ bit) for i in range(n)])


def copies_of(piece):
    return jnp.broadcast_to(piece[None], (lax.axis_size("cols"), *piece.shape))


def swap_cores(piece):
    return lax.ppermute(piece, "cols", [(i, i ^ 1) for i in range(lax.axis_size("cols"))])


def total(pieces):
    return jnp.sum(pieces.astype(F32), axis=0)


def join_body(*refs):
    *pieces, out_ref = refs
    at = 0
    for piece in pieces:
        out_ref[at : at + piece.shape[0]] = piece[...]
        at += piece.shape[0]


def join(pieces, weight):
    rows = sum(piece.shape[0] for piece in pieces)
    return pl.pallas_call(
        join_body,
        in_specs=[WHOLE] * len(pieces),
        out_specs=WHOLE,
        out_shape=jax.ShapeDtypeStruct((rows, pieces[0].shape[1]), pieces[0].dtype),
        compiler_params=pltpu.CompilerParams(vmem_limit_bytes=2 << 20),
        cost_estimate=pl.CostEstimate(flops=weight, transcendentals=0, bytes_accessed=0),
    )(*pieces)


def gather_rows(piece, weight=0):
    held = [piece]
    bit = lax.axis_size("rows") // 2
    while bit:
        whole = join(held, weight) if weight and bit == 1 else jnp.concatenate(held)
        held.append(swap(whole, bit))
        bit //= 2
    return held


def reduce_rows(near, far):
    bit = lax.axis_size("rows") // 2
    half = near.shape[0]
    got = swap(far, bit).astype(F32)
    kept = near.astype(F32) + got[:half]
    extra = far[half:].astype(F32) + got[half:]
    while bit > 1:
        bit //= 2
        kept, extra = kept.astype(BF16), extra.astype(BF16)
        half //= 2
        got_extra = swap(extra, bit)
        kept = kept[:half].astype(F32) + swap(kept[half:], bit).astype(F32)
        extra = extra.astype(F32) + got_extra.astype(F32)
    return kept, extra.astype(BF16)


def local(counts, start_a, start_b, start_c):
    rows_here, flat_width = counts.shape
    depth, rank = start_c.shape
    cols_here = flat_width // depth
    n_rows, n_cols = lax.axis_size("rows"), lax.axis_size("cols")
    total_i = rows_here * n_rows
    total_j = cols_here * n_cols
    rate_a = 0.3 / math.sqrt(total_j * depth)
    rate_b = 0.3 / math.sqrt(total_i * depth)
    rate_c = 0.3 / math.sqrt(total_i * total_j)
    counts = pltpu.with_memory_space_constraint(counts, pltpu.HBM)
    local_a, local_b = start_a, start_b
    rows_a, rows_b = start_a.shape[0], start_b.shape[0]
    shape_a = (n_cols, rows_a, rank)
    copies, low_b, c = prepare(start_a, start_b, start_c)
    for _ in range(ITERS - 1):
        got = lax.all_to_all(copies, "cols", 0, 0)
        assert got.shape == shape_a
        half = cols_here // 2
        pieces_a, near_b, far_b = call(
            first_body, counts, [got, *gather_rows(low_b), c],
            [(shape_a, BF16), ((half, rank), BF16), ((half + depth, rank), BF16)],
        )
        part_b, low_c = reduce_rows(near_b, far_b)
        got = lax.all_to_all(pieces_a, "cols", 0, 0)
        copies, low_b, local_a, local_b = update(
            got, local_a, part_b, local_b, low_c, rate_a, rate_b
        )
    got = lax.all_to_all(copies, "cols", 0, 0)
    b_parts = gather_rows(low_b, JOIN_WEIGHT)
    shape_half = (n_cols // 2, rows_a, rank)
    own_a, other_a, pieces_b, c = call(
        functools.partial(last_body, rate_c), counts, [got, *b_parts, c],
        [(shape_half, BF16)] * 2
        + [((n_rows, rows_b + depth, rank), BF16), (c.shape, F32)],
    )
    half_a = (own_a.astype(F32) + swap_cores(other_a).astype(F32)).astype(BF16)
    pieces_b, half_a = lax.optimization_barrier((pieces_b, half_a))
    part_b = total(lax.all_to_all(pieces_b, "rows", 0, 0))
    part_c = jnp.broadcast_to(part_b[None, rows_b:].astype(BF16), (n_cols // 2, depth, rank))
    same_core = [list(range(core, n_cols, 2)) for core in range(2)]
    sums = lax.all_to_all(
        jnp.concatenate([half_a, part_c], axis=1), "cols", 0, 0, axis_index_groups=same_core
    )
    sums, part_b = lax.optimization_barrier((sums, part_b))
    sums = total(sums)
    part_c = sums[rows_a:] + swap_cores(sums[rows_a:])
    return (
        local_a - rate_a * sums[:rows_a],
        local_b - rate_b * part_b[:rows_b],
        c - rate_c * part_c,
    )


def solution(mesh):
    placed = (P("rows", "cols"), P(("rows", "cols"), None), P(("cols", "rows"), None), P())
    return jax.shard_map(
        local,
        mesh=mesh,
        in_specs=placed,
        out_specs=(P(("rows", "cols"), None), P(("cols", "rows"), None), P()),
        check_vma=False,
    )
```

```python
import functools
import math

import jax
import jax.numpy as jnp
from jax import lax
from jax.experimental import pallas as pl
from jax.experimental.pallas import tpu as pltpu
from jax.sharding import PartitionSpec as P

ITERS = 2
BF16 = jnp.bfloat16
F32 = jnp.float32
WAITS = {0: (0,), 1: (1, 2), 4: (3,)}
JOIN_WEIGHT = 3_000_000_000
WHOLE = pl.BlockSpec(memory_space=pltpu.VMEM)


def prepare_body(a_ref, b_ref, c_ref, copies_ref, low_b_ref, held_c_ref, a_buf, b_buf, sems):
    into = ((a_ref, a_buf), (b_ref, b_buf), (c_ref, held_c_ref))
    moves = [pltpu.make_async_copy(src, dst, sems.at[k]) for k, (src, dst) in enumerate(into)]
    for move in moves:
        move.start()
    moves[1].wait()
    low_b_ref[...] = b_buf[...].astype(BF16)
    moves[0].wait()
    copies_ref[...] = jnp.broadcast_to(a_buf[...].astype(BF16)[None], copies_ref.shape)
    moves[2].wait()


def prepare(a, b, c):
    operands = [pltpu.with_memory_space_constraint(x, pltpu.HBM) for x in (a, b, c)]
    return pl.pallas_call(
        prepare_body,
        in_specs=[pl.BlockSpec(memory_space=pltpu.HBM)] * 3,
        out_specs=[WHOLE] * 3,
        out_shape=[
            jax.ShapeDtypeStruct((lax.axis_size("cols"), *a.shape), BF16),
            jax.ShapeDtypeStruct(b.shape, BF16),
            jax.ShapeDtypeStruct(c.shape, F32),
        ],
        scratch_shapes=[
            pltpu.VMEM(a.shape, F32),
            pltpu.VMEM(b.shape, F32),
            pltpu.SemaphoreType.DMA((3,)),
        ],
        compiler_params=pltpu.CompilerParams(vmem_limit_bytes=2 << 20),
    )(*operands)


def update_body(rate_a, rate_b, got_ref, a_ref, sum_b_ref, b_ref, low_c_ref, *outs):
    copies_ref, low_b_ref, new_a_ref, new_b_ref = outs
    new_b = b_ref[...] - rate_b * sum_b_ref[...]
    new_b_ref[...] = new_b
    low_b_ref[...] = new_b.astype(BF16)
    new_a = a_ref[...] - rate_a * total(got_ref[...])
    new_a_ref[...] = new_a
    parts, height, rank = copies_ref.shape
    rows = new_a.shape[0]
    copies_ref[:, :rows] = jnp.broadcast_to(new_a.astype(BF16)[None], (parts, rows, rank))
    copies_ref[:, rows:] = jnp.broadcast_to(low_c_ref[...][None], (parts, height - rows, rank))


def update(got, a, sum_b, b, low_c, rate_a, rate_b):
    parts, rows, rank = got.shape
    return pl.pallas_call(
        functools.partial(update_body, rate_a, rate_b),
        in_specs=[WHOLE] * 5,
        out_specs=[WHOLE] * 4,
        out_shape=[
            jax.ShapeDtypeStruct((parts, rows + low_c.shape[0], rank), BF16),
            jax.ShapeDtypeStruct(b.shape, BF16),
            jax.ShapeDtypeStruct(a.shape, F32),
            jax.ShapeDtypeStruct(b.shape, F32),
        ],
        compiler_params=pltpu.CompilerParams(vmem_limit_bytes=2 << 20),
    )(got, a, sum_b, b, low_c)


def visit_blocks(n_ref, held_ref, sems, low_a, b_of, c, put_b, acc_ref, grad_c):
    depth, rank = c.shape
    blocks = lax.axis_size("rows")
    me = lax.axis_index("rows")
    tile = n_ref.shape[1] // blocks
    wide = tile // depth

    def fetch(level):
        count = max(1 << level >> 1, 1)
        first = (me ^ (1 << level >> 1)) // count * count
        columns = pl.ds(pl.multiple_of(first * tile, tile), count * tile)
        return pltpu.make_async_copy(n_ref.at[:, columns], held_ref.at[:, columns], sems.at[level])

    levels = blocks.bit_length()
    for level in range(levels):
        fetch(level).start()
    for p in range(blocks):
        columns = pl.ds(pl.multiple_of((me ^ p) * tile, tile), tile)
        low_b = b_of(p).astype(F32)
        scaled = (low_b[:, None, :] * c[None]).astype(BF16).reshape(tile, rank)
        log_rate = lax.dot_general(
            low_a, scaled, (((1,), (1,)), ((), ())), preferred_element_type=F32
        )
        for level in WAITS.get(p, ()):
            fetch(level).wait()
        residual = (jnp.exp(log_rate) - held_ref[:, columns].astype(F32)).astype(BF16)
        mixed = lax.dot_general(
            residual, low_a, (((0,), (0,)), ((), ())), preferred_element_type=F32
        ).reshape(wide, depth, rank)
        put_b(p, jnp.sum(mixed * c[None], axis=1).astype(BF16))
        grad_c = grad_c + jnp.sum(mixed * low_b[:, None, :], axis=0)
        acc_ref[...] += jnp.dot(residual, scaled, preferred_element_type=F32)
    return grad_c


def parts_of(b_refs, wide):
    def b_of(x):
        steps = len(b_refs) - 1
        p = sum((x >> k & 1) << (steps - 1 - k) for k in range(steps))
        step = p.bit_length()
        start = (p - (1 << step >> 1)) * wide
        return b_refs[step][start : start + wide]

    return b_of


def first_body(n_ref, a_ref, *refs):
    b_refs, (c_ref, xa_ref, near_ref, far_ref, acc_ref, held_ref, sems) = refs[:-7], refs[-7:]
    blocks = lax.axis_size("rows")
    half = near_ref.shape[0]
    wide = 2 * half // blocks

    def put_b(p, value):
        at = p * wide % half
        (near_ref if p < blocks // 2 else far_ref)[at : at + wide] = value

    low_a = a_ref[...].reshape(acc_ref.shape)
    acc_ref[...] = jnp.zeros_like(acc_ref)
    b_of = parts_of(b_refs, wide)
    grad_c = jnp.zeros(c_ref.shape, F32)
    grad_c = visit_blocks(
        n_ref, held_ref, sems, low_a, b_of, c_ref[...], put_b, acc_ref, grad_c
    )
    xa_ref[...] = acc_ref[...].astype(BF16).reshape(xa_ref.shape)
    far_ref[half:] = grad_c.astype(BF16)


def last_body(rate_c, n_ref, got_ref, *refs):
    b_refs, rest = refs[:-8], refs[-8:]
    c_ref, own_ref, other_ref, xb_ref, new_c_ref, acc_ref, held_ref, sems = rest
    blocks = lax.axis_size("rows")
    me = lax.axis_index("rows")
    core = lax.axis_index("cols") % 2
    wide = xb_ref.shape[1]
    chips, rows = got_ref.shape[0] // 2, own_ref.shape[1]

    def put_b(x, value):
        xb_ref[me ^ x] = value

    acc_ref[...] = jnp.zeros_like(acc_ref)
    low_a = got_ref[:, :rows].reshape(acc_ref.shape)
    c = c_ref[...] - rate_c * total(got_ref[:, rows:])
    new_c_ref[...] = c
    b_of = parts_of(b_refs, wide)
    grad_c = jnp.zeros(c.shape, F32)
    grad_c = visit_blocks(
        n_ref, held_ref, sems, low_a, b_of, c, put_b, acc_ref, grad_c
    )
    for chip in range(chips):
        for piece_ref, which in ((own_ref, core), (other_ref, 1 - core)):
            at = pl.multiple_of((2 * chip + which) * rows, rows)
            piece_ref[chip] = acc_ref[pl.ds(at, rows)].astype(BF16)
    for piece_ref in (own_ref, other_ref):
        piece_ref[chips] = grad_c.astype(BF16)


def finish_body(rates, got_ref, part_b_ref, a_ref, b_ref, c_ref, out_a_ref, out_b_ref, out_c_ref):
    rows_a, rows_b = out_a_ref.shape[0], out_b_ref.shape[0]
    sums = total(got_ref[...])
    out_a_ref[...] = a_ref[...] - rates[0] * sums[:rows_a]
    out_b_ref[...] = b_ref[...] - rates[1] * part_b_ref[:rows_b]
    out_c_ref[...] = c_ref[...] - rates[2] * sums[rows_a:]


def finish(rates, got, part_b, *factors):
    return pl.pallas_call(
        functools.partial(finish_body, rates),
        in_specs=[WHOLE] * 5,
        out_specs=[WHOLE] * 3,
        out_shape=[jax.ShapeDtypeStruct(x.shape, F32) for x in factors],
        compiler_params=pltpu.CompilerParams(vmem_limit_bytes=2 << 20),
    )(got, part_b, *factors)


def call(body, counts, operands, outs):
    rows, flat = counts.shape
    rank = operands[0].shape[-1]
    return pl.pallas_call(
        body,
        in_specs=[pl.BlockSpec(memory_space=pltpu.HBM)] + [WHOLE] * len(operands),
        out_specs=[WHOLE] * len(outs),
        out_shape=[jax.ShapeDtypeStruct(shape, dtype) for shape, dtype in outs],
        scratch_shapes=[
            pltpu.VMEM((rows, rank), F32),
            pltpu.VMEM((rows, flat), BF16),
            pltpu.SemaphoreType.DMA((lax.axis_size("rows").bit_length(),)),
        ],
        compiler_params=pltpu.CompilerParams(vmem_limit_bytes=32 << 20),
        cost_estimate=pl.CostEstimate(
            flops=6 * rows * flat * rank,
            transcendentals=rows * flat,
            bytes_accessed=2 * rows * flat,
        ),
    )(counts, *operands)


def swap(piece, bit):
    n = lax.axis_size("rows")
    return lax.ppermute(piece, "rows", [(i, i ^ bit) for i in range(n)])


def swap_cores(piece):
    return lax.ppermute(piece, "cols", [(i, i ^ 1) for i in range(lax.axis_size("cols"))])


def exchange_chips(pieces):
    n = lax.axis_size("cols")
    groups = [list(range(core, n, 2)) for core in range(2)]
    return lax.all_to_all(pieces, "cols", 0, 0, axis_index_groups=groups)


def total(pieces):
    return jnp.sum(pieces.astype(F32), axis=0)


def join_body(*refs):
    *pieces, out_ref = refs
    at = 0
    for piece in pieces:
        out_ref[at : at + piece.shape[0]] = piece[...]
        at += piece.shape[0]


def join(pieces, weight):
    rows = sum(piece.shape[0] for piece in pieces)
    return pl.pallas_call(
        join_body,
        in_specs=[WHOLE] * len(pieces),
        out_specs=WHOLE,
        out_shape=jax.ShapeDtypeStruct((rows, pieces[0].shape[1]), pieces[0].dtype),
        compiler_params=pltpu.CompilerParams(vmem_limit_bytes=2 << 20),
        cost_estimate=pl.CostEstimate(flops=weight, transcendentals=0, bytes_accessed=0),
    )(*pieces)


def gather_rows(piece, weight=0):
    held = [piece]
    bit = lax.axis_size("rows") // 2
    while bit:
        whole = join(held, weight) if weight and bit == 1 else jnp.concatenate(held)
        held.append(swap(whole, bit))
        bit //= 2
    return held


def reduce_rows(near, far):
    bit = lax.axis_size("rows") // 2
    half = near.shape[0]
    got = swap(far, bit).astype(F32)
    kept = near.astype(F32) + got[:half]
    extra = far[half:].astype(F32) + got[half:]
    while bit > 1:
        bit //= 2
        kept, extra = kept.astype(BF16), extra.astype(BF16)
        half //= 2
        got_extra = swap(extra, bit)
        kept = kept[:half].astype(F32) + swap(kept[half:], bit).astype(F32)
        extra = extra.astype(F32) + got_extra.astype(F32)
    return kept, extra.astype(BF16)


def local(counts, start_a, start_b, start_c):
    rows_here, flat_width = counts.shape
    depth, rank = start_c.shape
    cols_here = flat_width // depth
    n_rows, n_cols = lax.axis_size("rows"), lax.axis_size("cols")
    total_i = rows_here * n_rows
    total_j = cols_here * n_cols
    rate_a = 0.3 / math.sqrt(total_j * depth)
    rate_b = 0.3 / math.sqrt(total_i * depth)
    rate_c = 0.3 / math.sqrt(total_i * total_j)
    counts = pltpu.with_memory_space_constraint(counts, pltpu.HBM)
    local_a, local_b = start_a, start_b
    rows_a, rows_b = start_a.shape[0], start_b.shape[0]
    shape_a = (n_cols, rows_a, rank)
    copies, low_b, c = prepare(start_a, start_b, start_c)
    for _ in range(ITERS - 1):
        got = lax.all_to_all(copies, "cols", 0, 0)
        assert got.shape == shape_a
        half = cols_here // 2
        pieces_a, near_b, far_b = call(
            first_body, counts, [got, *gather_rows(low_b), c],
            [(shape_a, BF16), ((half, rank), BF16), ((half + depth, rank), BF16)],
        )
        part_b, low_c = reduce_rows(near_b, far_b)
        got = lax.all_to_all(pieces_a, "cols", 0, 0)
        copies, low_b, local_a, local_b = update(
            got, local_a, part_b, local_b, low_c, rate_a, rate_b
        )
    got = lax.all_to_all(copies, "cols", 0, 0)
    b_parts = gather_rows(low_b, JOIN_WEIGHT)
    shape_half = (n_cols // 2 + 1, rows_a, rank)
    own, other, pieces_b, c = call(
        functools.partial(last_body, rate_c), counts, [got, *b_parts, c],
        [(shape_half, BF16)] * 2 + [((n_rows, rows_b, rank), BF16), (c.shape, F32)],
    )
    own = (own.astype(F32) + swap_cores(other).astype(F32)).astype(BF16)
    low_c = jnp.broadcast_to(own[-1:], (n_rows, depth, rank))
    pieces_b = jnp.concatenate([pieces_b, low_c], axis=1)
    pieces_b, half_a = lax.optimization_barrier((pieces_b, own[:-1]))
    part_b = total(lax.all_to_all(pieces_b, "rows", 0, 0))
    low_c = jnp.broadcast_to(part_b[None, rows_b:].astype(BF16), (n_cols // 2, depth, rank))
    got = exchange_chips(jnp.concatenate([half_a, low_c], axis=1))
    return tuple(finish((rate_a, rate_b, rate_c), got, part_b, local_a, local_b, c))


def solution(mesh):
    placed = (P("rows", "cols"), P(("rows", "cols"), None), P(("cols", "rows"), None), P())
    return jax.shard_map(
        local,
        mesh=mesh,
        in_specs=placed,
        out_specs=(P(("rows", "cols"), None), P(("cols", "rows"), None), P()),
        check_vma=False,
    )
```

```python
import functools
import math

import jax
import jax.numpy as jnp
from jax import lax
from jax.experimental import pallas as pl
from jax.experimental.pallas import tpu as pltpu
from jax.sharding import PartitionSpec as P

ITERS = 2
BF16 = jnp.bfloat16
F32 = jnp.float32
WAITS = {0: (0,), 1: (1, 2), 4: (3,)}
JOIN_WEIGHT = 3_000_000_000
WHOLE = pl.BlockSpec(memory_space=pltpu.VMEM)


def prepare_body(a_ref, b_ref, c_ref, copies_ref, low_b_ref, held_c_ref, a_buf, b_buf, sems):
    into = ((a_ref, a_buf), (b_ref, b_buf), (c_ref, held_c_ref))
    moves = [pltpu.make_async_copy(src, dst, sems.at[k]) for k, (src, dst) in enumerate(into)]
    for move in moves:
        move.start()
    moves[1].wait()
    low_b_ref[...] = b_buf[...].astype(BF16)
    moves[0].wait()
    copies_ref[...] = jnp.broadcast_to(a_buf[...].astype(BF16)[None], copies_ref.shape)
    moves[2].wait()


def prepare(a, b, c):
    operands = [pltpu.with_memory_space_constraint(x, pltpu.HBM) for x in (a, b, c)]
    return pl.pallas_call(
        prepare_body,
        in_specs=[pl.BlockSpec(memory_space=pltpu.HBM)] * 3,
        out_specs=[WHOLE] * 3,
        out_shape=[
            jax.ShapeDtypeStruct((lax.axis_size("cols"), *a.shape), BF16),
            jax.ShapeDtypeStruct(b.shape, BF16),
            jax.ShapeDtypeStruct(c.shape, F32),
        ],
        scratch_shapes=[
            pltpu.VMEM(a.shape, F32),
            pltpu.VMEM(b.shape, F32),
            pltpu.SemaphoreType.DMA((3,)),
        ],
        compiler_params=pltpu.CompilerParams(vmem_limit_bytes=2 << 20),
    )(*operands)


def update_body(rate_a, rate_b, got_ref, a_ref, sum_b_ref, b_ref, low_c_ref, *outs):
    copies_ref, low_b_ref, new_a_ref, new_b_ref = outs
    new_b = b_ref[...] - rate_b * sum_b_ref[...]
    new_b_ref[...] = new_b
    low_b_ref[...] = new_b.astype(BF16)
    new_a = a_ref[...] - rate_a * total(got_ref[...])
    new_a_ref[...] = new_a
    parts, height, rank = copies_ref.shape
    rows = new_a.shape[0]
    copies_ref[:, :rows] = jnp.broadcast_to(new_a.astype(BF16)[None], (parts, rows, rank))
    copies_ref[:, rows:] = jnp.broadcast_to(low_c_ref[...][None], (parts, height - rows, rank))


def update(got, a, sum_b, b, low_c, rate_a, rate_b):
    parts, rows, rank = got.shape
    return pl.pallas_call(
        functools.partial(update_body, rate_a, rate_b),
        in_specs=[WHOLE] * 5,
        out_specs=[WHOLE] * 4,
        out_shape=[
            jax.ShapeDtypeStruct((parts, rows + low_c.shape[0], rank), BF16),
            jax.ShapeDtypeStruct(b.shape, BF16),
            jax.ShapeDtypeStruct(a.shape, F32),
            jax.ShapeDtypeStruct(b.shape, F32),
        ],
        compiler_params=pltpu.CompilerParams(vmem_limit_bytes=2 << 20),
    )(got, a, sum_b, b, low_c)


def visit_blocks(n_ref, held_ref, sems, low_a, b_of, c, put_b, acc_ref, grad_c):
    depth, rank = c.shape
    blocks = lax.axis_size("rows")
    me = lax.axis_index("rows")
    tile = n_ref.shape[1] // blocks
    wide = tile // depth

    def fetch(level):
        count = max(1 << level >> 1, 1)
        first = (me ^ (1 << level >> 1)) // count * count
        columns = pl.ds(pl.multiple_of(first * tile, tile), count * tile)
        return pltpu.make_async_copy(n_ref.at[:, columns], held_ref.at[:, columns], sems.at[level])

    levels = blocks.bit_length()
    for level in range(levels):
        fetch(level).start()
    for p in range(blocks):
        columns = pl.ds(pl.multiple_of((me ^ p) * tile, tile), tile)
        low_b = b_of(p).astype(F32)
        scaled = (low_b[:, None, :] * c[None]).astype(BF16).reshape(tile, rank)
        log_rate = lax.dot_general(
            low_a, scaled, (((1,), (1,)), ((), ())), preferred_element_type=F32
        )
        for level in WAITS.get(p, ()):
            fetch(level).wait()
        residual = (jnp.exp(log_rate) - held_ref[:, columns].astype(F32)).astype(BF16)
        mixed = lax.dot_general(
            residual, low_a, (((0,), (0,)), ((), ())), preferred_element_type=F32
        ).reshape(wide, depth, rank)
        put_b(p, jnp.sum(mixed * c[None], axis=1).astype(BF16))
        grad_c = grad_c + jnp.sum(mixed * low_b[:, None, :], axis=0)
        acc_ref[...] += jnp.dot(residual, scaled, preferred_element_type=F32)
    return grad_c


def parts_of(b_refs, wide):
    def b_of(x):
        step = x.bit_length()
        start = (x - (1 << step >> 1)) * wide
        return b_refs[step][start : start + wide]

    return b_of


def first_body(n_ref, a_ref, *refs):
    b_refs, (c_ref, xa_ref, near_ref, far_ref, acc_ref, held_ref, sems) = refs[:-7], refs[-7:]
    blocks = lax.axis_size("rows")
    half = near_ref.shape[0]
    wide = 2 * half // blocks

    def put_b(p, value):
        at = p * wide % half
        (near_ref if p < blocks // 2 else far_ref)[at : at + wide] = value

    low_a = a_ref[...].reshape(acc_ref.shape)
    acc_ref[...] = jnp.zeros_like(acc_ref)
    b_of = parts_of(b_refs, wide)
    grad_c = jnp.zeros(c_ref.shape, F32)
    grad_c = visit_blocks(
        n_ref, held_ref, sems, low_a, b_of, c_ref[...], put_b, acc_ref, grad_c
    )
    xa_ref[...] = acc_ref[...].astype(BF16).reshape(xa_ref.shape)
    far_ref[half:] = grad_c.astype(BF16)


def last_body(rate_c, n_ref, got_ref, *refs):
    b_refs, rest = refs[:-8], refs[-8:]
    c_ref, own_ref, other_ref, xb_ref, new_c_ref, acc_ref, held_ref, sems = rest
    blocks = lax.axis_size("rows")
    me = lax.axis_index("rows")
    core = lax.axis_index("cols") % 2
    wide = xb_ref.shape[1]
    chips, rows = got_ref.shape[0] // 2, own_ref.shape[1]

    def put_b(x, value):
        xb_ref[me ^ x] = value

    acc_ref[...] = jnp.zeros_like(acc_ref)
    low_a = got_ref[:, :rows].reshape(acc_ref.shape)
    c = c_ref[...] - rate_c * total(got_ref[:, rows:])
    new_c_ref[...] = c
    b_of = parts_of(b_refs, wide)
    grad_c = jnp.zeros(c.shape, F32)
    grad_c = visit_blocks(
        n_ref, held_ref, sems, low_a, b_of, c, put_b, acc_ref, grad_c
    )
    for chip in range(chips):
        for piece_ref, which in ((own_ref, core), (other_ref, 1 - core)):
            at = pl.multiple_of((2 * chip + which) * rows, rows)
            piece_ref[chip] = acc_ref[pl.ds(at, rows)].astype(BF16)
    for piece_ref in (own_ref, other_ref):
        piece_ref[chips] = grad_c.astype(BF16)


def finish_body(rates, got_ref, part_b_ref, a_ref, b_ref, c_ref, out_a_ref, out_b_ref, out_c_ref):
    rows_a, rows_b = out_a_ref.shape[0], out_b_ref.shape[0]
    sums = total(got_ref[...])
    out_a_ref[...] = a_ref[...] - rates[0] * sums[:rows_a]
    out_b_ref[...] = b_ref[...] - rates[1] * part_b_ref[:rows_b]
    out_c_ref[...] = c_ref[...] - rates[2] * sums[rows_a:]


def finish(rates, got, part_b, *factors):
    return pl.pallas_call(
        functools.partial(finish_body, rates),
        in_specs=[WHOLE] * 5,
        out_specs=[WHOLE] * 3,
        out_shape=[jax.ShapeDtypeStruct(x.shape, F32) for x in factors],
        compiler_params=pltpu.CompilerParams(vmem_limit_bytes=2 << 20),
    )(got, part_b, *factors)


def call(body, counts, operands, outs):
    rows, flat = counts.shape
    rank = operands[0].shape[-1]
    return pl.pallas_call(
        body,
        in_specs=[pl.BlockSpec(memory_space=pltpu.HBM)] + [WHOLE] * len(operands),
        out_specs=[WHOLE] * len(outs),
        out_shape=[jax.ShapeDtypeStruct(shape, dtype) for shape, dtype in outs],
        scratch_shapes=[
            pltpu.VMEM((rows, rank), F32),
            pltpu.VMEM((rows, flat), BF16),
            pltpu.SemaphoreType.DMA((lax.axis_size("rows").bit_length(),)),
        ],
        compiler_params=pltpu.CompilerParams(vmem_limit_bytes=32 << 20),
        cost_estimate=pl.CostEstimate(
            flops=6 * rows * flat * rank,
            transcendentals=rows * flat,
            bytes_accessed=2 * rows * flat,
        ),
    )(counts, *operands)


def swap(piece, bit):
    n = lax.axis_size("rows")
    return lax.ppermute(piece, "rows", [(i, i ^ bit) for i in range(n)])


def swap_cores(piece):
    return lax.ppermute(piece, "cols", [(i, i ^ 1) for i in range(lax.axis_size("cols"))])


def exchange_chips(pieces):
    n = lax.axis_size("cols")
    groups = [list(range(core, n, 2)) for core in range(2)]
    return lax.all_to_all(pieces, "cols", 0, 0, axis_index_groups=groups)


def total(pieces):
    return jnp.sum(pieces.astype(F32), axis=0)


def join_body(*refs):
    *pieces, out_ref = refs
    at = 0
    for piece in pieces:
        out_ref[at : at + piece.shape[0]] = piece[...]
        at += piece.shape[0]


def join(pieces, weight):
    rows = sum(piece.shape[0] for piece in pieces)
    return pl.pallas_call(
        join_body,
        in_specs=[WHOLE] * len(pieces),
        out_specs=WHOLE,
        out_shape=jax.ShapeDtypeStruct((rows, pieces[0].shape[1]), pieces[0].dtype),
        compiler_params=pltpu.CompilerParams(vmem_limit_bytes=2 << 20),
        cost_estimate=pl.CostEstimate(flops=weight, transcendentals=0, bytes_accessed=0),
    )(*pieces)


def gather_rows(piece, weight=0):
    n = lax.axis_size("rows")
    held = [piece]
    bit = 1
    while bit < n:
        whole = join(held, weight) if weight and 2 * bit == n else jnp.concatenate(held)
        held.append(swap(whole, bit))
        bit *= 2
    return held


def reduce_rows(near, far):
    bit = lax.axis_size("rows") // 2
    half = near.shape[0]
    got = swap(far, bit).astype(F32)
    kept = near.astype(F32) + got[:half]
    extra = far[half:].astype(F32) + got[half:]
    while bit > 1:
        bit //= 2
        kept, extra = kept.astype(BF16), extra.astype(BF16)
        half //= 2
        got_extra = swap(extra, bit)
        kept = kept[:half].astype(F32) + swap(kept[half:], bit).astype(F32)
        extra = extra.astype(F32) + got_extra.astype(F32)
    return kept, extra.astype(BF16)


def local(counts, start_a, start_b, start_c):
    rows_here, flat_width = counts.shape
    depth, rank = start_c.shape
    cols_here = flat_width // depth
    n_rows, n_cols = lax.axis_size("rows"), lax.axis_size("cols")
    total_i = rows_here * n_rows
    total_j = cols_here * n_cols
    rate_a = 0.3 / math.sqrt(total_j * depth)
    rate_b = 0.3 / math.sqrt(total_i * depth)
    rate_c = 0.3 / math.sqrt(total_i * total_j)
    counts = pltpu.with_memory_space_constraint(counts, pltpu.HBM)
    local_a, local_b = start_a, start_b
    rows_a, rows_b = start_a.shape[0], start_b.shape[0]
    shape_a = (n_cols, rows_a, rank)
    copies, low_b, c = prepare(start_a, start_b, start_c)
    for _ in range(ITERS - 1):
        got = lax.all_to_all(copies, "cols", 0, 0)
        assert got.shape == shape_a
        half = cols_here // 2
        pieces_a, near_b, far_b = call(
            first_body, counts, [got, *gather_rows(low_b), c],
            [(shape_a, BF16), ((half, rank), BF16), ((half + depth, rank), BF16)],
        )
        part_b, low_c = reduce_rows(near_b, far_b)
        got = lax.all_to_all(pieces_a, "cols", 0, 0)
        copies, low_b, local_a, local_b = update(
            got, local_a, part_b, local_b, low_c, rate_a, rate_b
        )
    got = lax.all_to_all(copies, "cols", 0, 0)
    b_parts = gather_rows(low_b, JOIN_WEIGHT)
    shape_half = (n_cols // 2 + 1, rows_a, rank)
    own, other, pieces_b, c = call(
        functools.partial(last_body, rate_c), counts, [got, *b_parts, c],
        [(shape_half, BF16)] * 2 + [((n_rows, rows_b, rank), BF16), (c.shape, F32)],
    )
    own = (own.astype(F32) + swap_cores(other).astype(F32)).astype(BF16)
    low_c = jnp.broadcast_to(own[-1:], (n_rows, depth, rank))
    pieces_b = jnp.concatenate([pieces_b, low_c], axis=1)
    pieces_b, half_a = lax.optimization_barrier((pieces_b, own[:-1]))
    part_b = total(lax.all_to_all(pieces_b, "rows", 0, 0))
    low_c = jnp.broadcast_to(part_b[None, rows_b:].astype(BF16), (n_cols // 2, depth, rank))
    got = exchange_chips(jnp.concatenate([half_a, low_c], axis=1))
    return tuple(finish((rate_a, rate_b, rate_c), got, part_b, local_a, local_b, c))


def solution(mesh):
    placed = (P("rows", "cols"), P(("rows", "cols"), None), P(("cols", "rows"), None), P())
    return jax.shard_map(
        local,
        mesh=mesh,
        in_specs=placed,
        out_specs=(P(("rows", "cols"), None), P(("cols", "rows"), None), P()),
        check_vma=False,
    )
```

```python
import functools
import math

import jax
import jax.numpy as jnp
from jax import lax
from jax.experimental import pallas as pl
from jax.experimental.pallas import tpu as pltpu
from jax.sharding import PartitionSpec as P

ITERS = 2
BF16 = jnp.bfloat16
F32 = jnp.float32
WAITS = {0: (0,), 1: (1, 2), 4: (3,)}
JOIN_WEIGHT = 3_000_000_000
WHOLE = pl.BlockSpec(memory_space=pltpu.VMEM)


def prepare_body(a_ref, b_ref, c_ref, copies_ref, low_b_ref, held_c_ref, a_buf, b_buf, sems):
    into = ((a_ref, a_buf), (b_ref, b_buf), (c_ref, held_c_ref))
    moves = [pltpu.make_async_copy(src, dst, sems.at[k]) for k, (src, dst) in enumerate(into)]
    for move in moves:
        move.start()
    moves[1].wait()
    low_b_ref[...] = b_buf[...].astype(BF16)
    moves[0].wait()
    copies_ref[...] = jnp.broadcast_to(a_buf[...].astype(BF16)[None], copies_ref.shape)
    moves[2].wait()


def prepare(a, b, c):
    operands = [pltpu.with_memory_space_constraint(x, pltpu.HBM) for x in (a, b, c)]
    return pl.pallas_call(
        prepare_body,
        in_specs=[pl.BlockSpec(memory_space=pltpu.HBM)] * 3,
        out_specs=[WHOLE] * 3,
        out_shape=[
            jax.ShapeDtypeStruct((lax.axis_size("cols"), *a.shape), BF16),
            jax.ShapeDtypeStruct(b.shape, BF16),
            jax.ShapeDtypeStruct(c.shape, F32),
        ],
        scratch_shapes=[
            pltpu.VMEM(a.shape, F32),
            pltpu.VMEM(b.shape, F32),
            pltpu.SemaphoreType.DMA((3,)),
        ],
        compiler_params=pltpu.CompilerParams(vmem_limit_bytes=2 << 20),
    )(*operands)


def update_body(rate_a, rate_b, got_ref, a_ref, sum_b_ref, b_ref, low_c_ref, *outs):
    copies_ref, low_b_ref, new_a_ref, new_b_ref = outs
    new_b = b_ref[...] - rate_b * sum_b_ref[...]
    new_b_ref[...] = new_b
    low_b_ref[...] = new_b.astype(BF16)
    new_a = a_ref[...] - rate_a * total(got_ref[...])
    new_a_ref[...] = new_a
    parts, height, rank = copies_ref.shape
    rows = new_a.shape[0]
    copies_ref[:, :rows] = jnp.broadcast_to(new_a.astype(BF16)[None], (parts, rows, rank))
    copies_ref[:, rows:] = jnp.broadcast_to(low_c_ref[...][None], (parts, height - rows, rank))


def update(got, a, sum_b, b, low_c, rate_a, rate_b):
    parts, rows, rank = got.shape
    return pl.pallas_call(
        functools.partial(update_body, rate_a, rate_b),
        in_specs=[WHOLE] * 5,
        out_specs=[WHOLE] * 4,
        out_shape=[
            jax.ShapeDtypeStruct((parts, rows + low_c.shape[0], rank), BF16),
            jax.ShapeDtypeStruct(b.shape, BF16),
            jax.ShapeDtypeStruct(a.shape, F32),
            jax.ShapeDtypeStruct(b.shape, F32),
        ],
        compiler_params=pltpu.CompilerParams(vmem_limit_bytes=2 << 20),
    )(got, a, sum_b, b, low_c)


def visit_blocks(n_ref, held_ref, sems, low_a, b_of, c, put_b, acc_ref, grad_c):
    depth, rank = c.shape
    blocks = lax.axis_size("rows")
    me = lax.axis_index("rows")
    tile = n_ref.shape[1] // blocks
    wide = tile // depth

    def fetch(level):
        count = max(1 << level >> 1, 1)
        first = (me ^ (1 << level >> 1)) // count * count
        columns = pl.ds(pl.multiple_of(first * tile, tile), count * tile)
        return pltpu.make_async_copy(n_ref.at[:, columns], held_ref.at[:, columns], sems.at[level])

    levels = blocks.bit_length()
    for level in range(levels):
        fetch(level).start()
    for p in range(blocks):
        columns = pl.ds(pl.multiple_of((me ^ p) * tile, tile), tile)
        low_b = b_of(p).astype(F32)
        scaled = (low_b[:, None, :] * c[None]).astype(BF16).reshape(tile, rank)
        log_rate = lax.dot_general(
            low_a, scaled, (((1,), (1,)), ((), ())), preferred_element_type=F32
        )
        for level in WAITS.get(p, ()):
            fetch(level).wait()
        residual = (jnp.exp(log_rate) - held_ref[:, columns].astype(F32)).astype(BF16)
        mixed = lax.dot_general(
            residual, low_a, (((0,), (0,)), ((), ())), preferred_element_type=F32
        ).reshape(wide, depth, rank)
        put_b(p, jnp.sum(mixed * c[None], axis=1).astype(BF16))
        grad_c = grad_c + jnp.sum(mixed * low_b[:, None, :], axis=0)
        acc_ref[...] += jnp.dot(residual, scaled, preferred_element_type=F32)
    return grad_c


def parts_of(b_refs, wide, near):
    def b_of(x):
        steps = len(b_refs) - 1
        p = x if near else sum((x >> k & 1) << (steps - 1 - k) for k in range(steps))
        step = p.bit_length()
        start = (p - (1 << step >> 1)) * wide
        return b_refs[step][start : start + wide]

    return b_of


def first_body(n_ref, a_ref, *refs):
    b_refs, (c_ref, xa_ref, near_ref, far_ref, acc_ref, held_ref, sems) = refs[:-7], refs[-7:]
    blocks = lax.axis_size("rows")
    half = near_ref.shape[0]
    wide = 2 * half // blocks

    def put_b(p, value):
        at = p * wide % half
        (near_ref if p < blocks // 2 else far_ref)[at : at + wide] = value

    low_a = a_ref[...].reshape(acc_ref.shape)
    acc_ref[...] = jnp.zeros_like(acc_ref)
    b_of = parts_of(b_refs, wide, False)
    grad_c = jnp.zeros(c_ref.shape, F32)
    grad_c = visit_blocks(
        n_ref, held_ref, sems, low_a, b_of, c_ref[...], put_b, acc_ref, grad_c
    )
    xa_ref[...] = acc_ref[...].astype(BF16).reshape(xa_ref.shape)
    far_ref[half:] = grad_c.astype(BF16)


def last_body(rate_c, n_ref, got_ref, *refs):
    b_refs, rest = refs[:-8], refs[-8:]
    c_ref, own_ref, other_ref, xb_ref, new_c_ref, acc_ref, held_ref, sems = rest
    blocks = lax.axis_size("rows")
    me = lax.axis_index("rows")
    core = lax.axis_index("cols") % 2
    wide = xb_ref.shape[1]
    chips, rows = got_ref.shape[0] // 2, own_ref.shape[1]

    def put_b(x, value):
        xb_ref[me ^ x] = value

    acc_ref[...] = jnp.zeros_like(acc_ref)
    low_a = got_ref[:, :rows].reshape(acc_ref.shape)
    c = c_ref[...] - rate_c * total(got_ref[:, rows:])
    new_c_ref[...] = c
    b_of = parts_of(b_refs, wide, True)
    grad_c = jnp.zeros(c.shape, F32)
    grad_c = visit_blocks(
        n_ref, held_ref, sems, low_a, b_of, c, put_b, acc_ref, grad_c
    )
    for chip in range(chips):
        for piece_ref, which in ((own_ref, core), (other_ref, 1 - core)):
            at = pl.multiple_of((2 * chip + which) * rows, rows)
            piece_ref[chip] = acc_ref[pl.ds(at, rows)].astype(BF16)
    for piece_ref in (own_ref, other_ref):
        piece_ref[chips] = grad_c.astype(BF16)


def finish_body(rates, got_ref, part_b_ref, a_ref, b_ref, c_ref, out_a_ref, out_b_ref, out_c_ref):
    rows_a, rows_b = out_a_ref.shape[0], out_b_ref.shape[0]
    sums = total(got_ref[...])
    out_a_ref[...] = a_ref[...] - rates[0] * sums[:rows_a]
    out_b_ref[...] = b_ref[...] - rates[1] * part_b_ref[:rows_b]
    out_c_ref[...] = c_ref[...] - rates[2] * sums[rows_a:]


def finish(rates, got, part_b, *factors):
    return pl.pallas_call(
        functools.partial(finish_body, rates),
        in_specs=[WHOLE] * 5,
        out_specs=[WHOLE] * 3,
        out_shape=[jax.ShapeDtypeStruct(x.shape, F32) for x in factors],
        compiler_params=pltpu.CompilerParams(vmem_limit_bytes=2 << 20),
    )(got, part_b, *factors)


def call(body, counts, operands, outs):
    rows, flat = counts.shape
    rank = operands[0].shape[-1]
    return pl.pallas_call(
        body,
        in_specs=[pl.BlockSpec(memory_space=pltpu.HBM)] + [WHOLE] * len(operands),
        out_specs=[WHOLE] * len(outs),
        out_shape=[jax.ShapeDtypeStruct(shape, dtype) for shape, dtype in outs],
        scratch_shapes=[
            pltpu.VMEM((rows, rank), F32),
            pltpu.VMEM((rows, flat), BF16),
            pltpu.SemaphoreType.DMA((lax.axis_size("rows").bit_length(),)),
        ],
        compiler_params=pltpu.CompilerParams(vmem_limit_bytes=32 << 20),
        cost_estimate=pl.CostEstimate(
            flops=6 * rows * flat * rank,
            transcendentals=rows * flat,
            bytes_accessed=2 * rows * flat,
        ),
    )(counts, *operands)


def swap(piece, bit):
    n = lax.axis_size("rows")
    return lax.ppermute(piece, "rows", [(i, i ^ bit) for i in range(n)])


def swap_cores(piece):
    return lax.ppermute(piece, "cols", [(i, i ^ 1) for i in range(lax.axis_size("cols"))])


def exchange_chips(pieces):
    n = lax.axis_size("cols")
    groups = [list(range(core, n, 2)) for core in range(2)]
    return lax.all_to_all(pieces, "cols", 0, 0, axis_index_groups=groups)


def total(pieces):
    return jnp.sum(pieces.astype(F32), axis=0)


def join_body(*refs):
    *pieces, out_ref = refs
    at = 0
    for piece in pieces:
        out_ref[at : at + piece.shape[0]] = piece[...]
        at += piece.shape[0]


def join(pieces, weight):
    rows = sum(piece.shape[0] for piece in pieces)
    return pl.pallas_call(
        join_body,
        in_specs=[WHOLE] * len(pieces),
        out_specs=WHOLE,
        out_shape=jax.ShapeDtypeStruct((rows, pieces[0].shape[1]), pieces[0].dtype),
        compiler_params=pltpu.CompilerParams(vmem_limit_bytes=2 << 20),
        cost_estimate=pl.CostEstimate(flops=weight, transcendentals=0, bytes_accessed=0),
    )(*pieces)


def gather_rows(piece, near=False):
    steps = lax.axis_size("rows").bit_length() - 1
    held = [piece]
    for k in range(steps):
        whole = join(held, JOIN_WEIGHT) if near and k == steps - 1 else jnp.concatenate(held)
        held.append(swap(whole, 1 << (k if near else steps - 1 - k)))
    return held


def reduce_rows(near, far):
    bit = lax.axis_size("rows") // 2
    half = near.shape[0]
    got = swap(far, bit).astype(F32)
    kept = near.astype(F32) + got[:half]
    extra = far[half:].astype(F32) + got[half:]
    while bit > 1:
        bit //= 2
        kept, extra = kept.astype(BF16), extra.astype(BF16)
        half //= 2
        got_extra = swap(extra, bit)
        kept = kept[:half].astype(F32) + swap(kept[half:], bit).astype(F32)
        extra = extra.astype(F32) + got_extra.astype(F32)
    return kept, extra.astype(BF16)


def local(counts, start_a, start_b, start_c):
    rows_here, flat_width = counts.shape
    depth, rank = start_c.shape
    cols_here = flat_width // depth
    n_rows, n_cols = lax.axis_size("rows"), lax.axis_size("cols")
    total_i = rows_here * n_rows
    total_j = cols_here * n_cols
    rate_a = 0.3 / math.sqrt(total_j * depth)
    rate_b = 0.3 / math.sqrt(total_i * depth)
    rate_c = 0.3 / math.sqrt(total_i * total_j)
    counts = pltpu.with_memory_space_constraint(counts, pltpu.HBM)
    local_a, local_b = start_a, start_b
    rows_a, rows_b = start_a.shape[0], start_b.shape[0]
    shape_a = (n_cols, rows_a, rank)
    copies, low_b, c = prepare(start_a, start_b, start_c)
    for _ in range(ITERS - 1):
        got = lax.all_to_all(copies, "cols", 0, 0)
        assert got.shape == shape_a
        half = cols_here // 2
        pieces_a, near_b, far_b = call(
            first_body, counts, [got, *gather_rows(low_b), c],
            [(shape_a, BF16), ((half, rank), BF16), ((half + depth, rank), BF16)],
        )
        part_b, low_c = reduce_rows(near_b, far_b)
        got = lax.all_to_all(pieces_a, "cols", 0, 0)
        copies, low_b, local_a, local_b = update(
            got, local_a, part_b, local_b, low_c, rate_a, rate_b
        )
    got = lax.all_to_all(copies, "cols", 0, 0)
    b_parts = gather_rows(low_b, True)
    shape_half = (n_cols // 2 + 1, rows_a, rank)
    own, other, pieces_b, c = call(
        functools.partial(last_body, rate_c), counts, [got, *b_parts, c],
        [(shape_half, BF16)] * 2 + [((n_rows, rows_b, rank), BF16), (c.shape, F32)],
    )
    own = (own.astype(F32) + swap_cores(other).astype(F32)).astype(BF16)
    low_c = jnp.broadcast_to(own[-1:], (n_rows, depth, rank))
    pieces_b = jnp.concatenate([pieces_b, low_c], axis=1)
    pieces_b, half_a = lax.optimization_barrier((pieces_b, own[:-1]))
    part_b = total(lax.all_to_all(pieces_b, "rows", 0, 0))
    low_c = jnp.broadcast_to(part_b[None, rows_b:].astype(BF16), (n_cols // 2, depth, rank))
    got = exchange_chips(jnp.concatenate([half_a, low_c], axis=1))
    return tuple(finish((rate_a, rate_b, rate_c), got, part_b, local_a, local_b, c))


def solution(mesh):
    placed = (P("rows", "cols"), P(("rows", "cols"), None), P(("cols", "rows"), None), P())
    return jax.shard_map(
        local,
        mesh=mesh,
        in_specs=placed,
        out_specs=(P(("rows", "cols"), None), P(("cols", "rows"), None), P()),
        check_vma=False,
    )
```
